32 devices in a mesh: row: 8 (over y, x, core), rep: 4 (over z).
Axes of the slice: x: 2, y: 2, z: 4, core: 2. Of those that a mesh axis runs over, the one named last changes fastest.
Arguments:
- features: bfloat16 [8192, 512], P(('row', 'rep')), may hold values from -6 to 6
- tiles: bfloat16 [64, 8, 128, 128], P(('row', 'rep')), may hold values from -0.1875 to 0.1875
- columns: int32 [64, 8], P(('row', 'rep')), may hold values from 0 to 63, as said below
- w_aggregate: bfloat16 [512, 512], replicated, may hold values from -0.25 to 0.25
- w_self: bfloat16 [512, 512], replicated, may hold values from -0.25 to 0.25
- w_middle: bfloat16 [512, 512], replicated, may hold values from -0.25 to 0.25
- w_output: bfloat16 [512, 512], replicated, may hold values from -0.25 to 0.25
- cotangent: bfloat16 [8192, 512], P(('row', 'rep')), may hold values from -6 to 6
Outputs:
- updated: bfloat16 [8192, 512], P(('row', 'rep'))
- grad_features: bfloat16 [8192, 512], P(('row', 'rep'))
- grad_output: float32 [512, 512], P('rep')
- grad_middle: float32 [512, 512], P('rep')
- grad_aggregate: float32 [512, 512], P('rep')
- grad_self: float32 [512, 512], P('rep')
The draws below stay inside these ranges and needn't reach their ends.
Inputs may be any that keep to these rules, and one draw needn't show every extreme that they name: `columns`: row group g holds row blocks g * 8 to (g + 1) * 8 - 1, for g < 8. Every column block named by a row block of group g lies in group g - 1, g or g + 1, taken modulo 8; every row block names each of these three groups at least once. Column blocks may repeat within a row block.
All inputs are finite; a program needn't handle non-finite values.
Results may differ from the reference program's by a relative error of at most 0.015.
Values may be sent and summed in bfloat16 or wider, within the bound.
No kernel may reach another device: no remote copies, remote signals or barrier semaphores. Data moves between devices by JAX's collectives and lax.ppermute only.
A program may use at most 192 MiB of HBM per device.

```python
import jax
import jax.numpy as jnp

F = 512
TILE = 128
K = 8
GROUPS = 8
PANEL_BLOCKS = 8
BLOCKS = 64
NODES = 8192


def draw_columns(key, part):
    key_offset, key_within = jax.random.split(key)
    block_ids = jnp.arange(BLOCKS, dtype=jnp.int32)
    group_ids = block_ids // PANEL_BLOCKS
    random_offset = jax.random.randint(key_offset, (BLOCKS, K), -1, 2, dtype=jnp.int32)
    position = jnp.arange(K, dtype=jnp.int32)[None, :]
    offset = jnp.where(position == 0, -1, jnp.where(position == 1, 1, jnp.where(position == 2, 0, random_offset)))
    within = jax.random.randint(key_within, (BLOCKS, K), 0, PANEL_BLOCKS, dtype=jnp.int32)
    target = (group_ids[:, None] + offset + GROUPS) % GROUPS
    return (target * PANEL_BLOCKS + within).astype(jnp.int32)


def shard_levels(own_key, dims, shards, low, high):
    loudness = 1.0
    for dim, blocks in shards:
        steps = jax.random.uniform(jax.random.fold_in(jax.random.fold_in(own_key, 6), dim), (blocks,), jnp.float32, low / len(shards), high / len(shards))
        loudness = loudness * jnp.repeat(jnp.exp(steps), dims[dim] // blocks).reshape((-1,) + (1,) * (len(dims) - 1 - dim))
    return loudness


def gaussian(key, shape, scale, limit, cuts=(), kind=jnp.bfloat16):
    factor_of = shard_levels(key, shape, cuts, -0.22, 0.18) if cuts else 1.0
    result = jax.random.normal(key, shape, jnp.float32) * scale * factor_of
    return jnp.minimum(jnp.maximum(result, -limit), limit).astype(kind)


def setup_inputs(seed: int = 0) -> dict:
    streams_of = jax.random.split(jax.random.key(seed), 9)
    features = gaussian(streams_of[0], (NODES, F), 1.0, 6.0, ((0, 32),))
    tiles = gaussian(streams_of[1], (BLOCKS, K, TILE, TILE), (K * TILE) ** -0.5, 0.1875, ((0, 32),))
    columns = draw_columns(jax.random.fold_in(streams_of[8], 71), 0)
    w_aggregate = gaussian(streams_of[3], (F, F), F ** -0.5, 0.25)
    w_self = gaussian(streams_of[4], (F, F), F ** -0.5, 0.25)
    w_middle = gaussian(streams_of[5], (F, F), F ** -0.5, 0.25)
    w_output = gaussian(streams_of[6], (F, F), F ** -0.5, 0.25)
    cotangent = gaussian(streams_of[7], (NODES, F), 1.0, 6.0, ((0, 32),))
    return dict(features=features, tiles=tiles, columns=columns, w_aggregate=w_aggregate, w_self=w_self, w_middle=w_middle, w_output=w_output, cotangent=cotangent)


def silu_slope(value):
    sig = jax.nn.sigmoid(value)
    return sig * (1.0 + value * (1.0 - sig))


def reference(features, tiles, columns, w_aggregate, w_self, w_middle, w_output, cotangent):
    node_blocks = features.reshape(BLOCKS, TILE, F)
    summed = jnp.zeros((BLOCKS, TILE, F), jnp.float32)
    for column in range(K):
        picked = node_blocks[columns[:, column]].astype(jnp.float32)
        summed = summed + jnp.einsum("bij,bjf->bif", tiles[:, column].astype(jnp.float32), picked)
    aggregate = summed.reshape(NODES, F).astype(jnp.bfloat16)
    pre_first = jnp.dot(aggregate, w_aggregate, preferred_element_type=jnp.float32) + jnp.dot(features, w_self, preferred_element_type=jnp.float32)
    first = jax.nn.silu(pre_first).astype(jnp.bfloat16)
    pre_second = jnp.dot(first, w_middle, preferred_element_type=jnp.float32)
    second = jax.nn.silu(pre_second).astype(jnp.bfloat16)
    updated = (features.astype(jnp.float32) + jnp.dot(second, w_output, preferred_element_type=jnp.float32)).astype(jnp.bfloat16)
    delta_second = (jnp.dot(cotangent, w_output.T, preferred_element_type=jnp.float32) * silu_slope(pre_second)).astype(jnp.bfloat16)
    delta_first = (jnp.dot(delta_second, w_middle.T, preferred_element_type=jnp.float32) * silu_slope(pre_first)).astype(jnp.bfloat16)
    delta_aggregate = jnp.dot(delta_first, w_aggregate.T, preferred_element_type=jnp.float32).astype(jnp.bfloat16)
    delta_blocks = delta_aggregate.reshape(BLOCKS, TILE, F).astype(jnp.float32)
    returned = jnp.zeros((BLOCKS, TILE, F), jnp.float32)
    for column in range(K):
        message = jnp.einsum("bji,bjf->bif", tiles[:, column].astype(jnp.float32), delta_blocks)
        returned = returned.at[columns[:, column]].add(message)
    grad_features = (cotangent.astype(jnp.float32) + jnp.dot(delta_first, w_self.T, preferred_element_type=jnp.float32) + returned.reshape(NODES, F)).astype(jnp.bfloat16)
    scale = 1.0 / (NODES ** 0.5)
    grad_output = jnp.dot(second.T, cotangent, preferred_element_type=jnp.float32) * scale
    grad_middle = jnp.dot(first.T, delta_second, preferred_element_type=jnp.float32) * scale
    grad_aggregate = jnp.dot(aggregate.T, delta_first, preferred_element_type=jnp.float32) * scale
    grad_self = jnp.dot(features.T, delta_first, preferred_element_type=jnp.float32) * scale
    return (updated, grad_features, grad_output, grad_middle, grad_aggregate, grad_self)
```

```python
import math

import jax
import jax.numpy as jnp
from jax import lax
from jax.experimental import pallas as pl
from jax.experimental.pallas import tpu as pltpu
from jax.sharding import PartitionSpec as P


BF = jnp.bfloat16
F32 = jnp.float32
VM = pl.BlockSpec(memory_space=pltpu.VMEM)
SM = pl.BlockSpec(memory_space=pltpu.SMEM)


def swap(value, axis, flip):
    count = lax.axis_size(axis)
    return lax.ppermute(value, axis, [(i, i ^ flip) for i in range(count)])


def swap_off(value):
    count = lax.axis_size("row")
    pairs = [(i, (i + 1) % count if i % 2 else (i - 1) % count) for i in range(count)]
    return lax.ppermute(value, "row", pairs)


def nbytes(shape, dtype):
    return math.prod(shape) * jnp.dtype(dtype).itemsize


def call(body, name, outs, ins, specs=None, flops=0):
    moved = sum(nbytes(o[0], o[1]) for o in outs) + sum(nbytes(i.shape, i.dtype) for i in ins)
    return pl.pallas_call(
        body,
        name=name,
        out_shape=[jax.ShapeDtypeStruct(shape, dtype) for shape, dtype in outs],
        in_specs=specs or [VM] * len(ins),
        out_specs=[VM] * len(outs),
        compiler_params=pltpu.CompilerParams(
            vmem_limit_bytes=min(moved + (8 << 20), 60 << 20)
        ),
        cost_estimate=pl.CostEstimate(flops=flops, bytes_accessed=moved, transcendentals=0),
    )(*ins)


def dot(left, right):
    return jnp.dot(left, right, preferred_element_type=F32)


def dot_nt(left, right):
    return lax.dot_general(left, right, (((1,), (1,)), ((), ())), preferred_element_type=F32)


def dot_tn(left, right):
    return lax.dot_general(left, right, (((0,), (0,)), ((), ())), preferred_element_type=F32)


def local(features, tiles, columns, w_aggregate, w_self, w_middle, w_output, cotangent):
    blocks_dev, width_k, tile, _ = tiles.shape
    rows, width = features.shape
    half = width // 2
    groups = lax.axis_size("row")
    reps = lax.axis_size("rep")
    chips = groups // 2
    panel_blocks = reps * blocks_dev
    blocks = 3 * panel_blocks
    scale = 1.0 / math.sqrt(rows * groups * reps)
    level_rows = width // reps
    share_rows = 2 * level_rows // chips

    def half_of(offset):
        return pl.ds(pl.multiple_of(offset * half, half), half)

    def split_body(f_ref, mine_ref, other_ref):
        h = lax.axis_index("rep") & 1
        mine_ref[...] = f_ref[:, half_of(h)]
        other_ref[...] = f_ref[:, half_of(1 - h)]

    piece = ((rows, half), BF)
    own_mine, own_other = call(split_body, "split", [piece, piece], [features])

    own = [own_mine] + [None] * (reps - 1)
    for d in range(reps - 1, 0, -1):
        own[d] = swap(own_other if d & 1 else own_mine, "rep", d)
    pair_columns = swap(columns, "rep", 1)
    pair_tiles = swap(tiles, "rep", 1)
    near = [swap(v, "row", 1) for v in own]
    far = [swap_off(v) for v in own]

    def build_body(t_ref, c_ref, a_ref, at_ref):
        g = lax.axis_index("row")
        r = lax.axis_index("rep")
        a_ref[...] = jnp.zeros_like(a_ref)
        at_ref[...] = jnp.zeros_like(at_ref)
        for b in range(blocks_dev):
            for k in range(width_k):
                c = c_ref[b, k]
                within = lax.rem(c, panel_blocks)
                group = lax.div(c, panel_blocks)
                slot = jnp.where(group == g, 0, jnp.where(group == (g ^ 1), 1, 2))
                level = lax.div(within, blocks_dev) ^ r
                index = (slot * reps + level) * blocks_dev + lax.rem(within, blocks_dev)
                t = t_ref[b, k]
                here = pl.ds(b * tile, tile)
                a_ref[index, here, :] += t
                at_ref[index, :, here] += t.T

    adj_shapes = [((blocks, rows, tile), BF), ((blocks, tile, rows), BF)]
    a_own, at_own = call(build_body, "build_own", adj_shapes, [tiles, columns], [VM, SM])
    a_pair, at_pair = call(build_body, "build_pair", adj_shapes, [pair_tiles, pair_columns], [VM, SM])

    def early_body(f_ref, c_ref, ws_ref, wo_ref, self_ref, dso_ref):
        self_ref[...] = dot(f_ref[...], ws_ref[...])
        dso_ref[...] = dot_nt(c_ref[...], wo_ref[...])

    flops = 2 * rows * width * width
    wide = ((rows, width), F32)
    from_self, from_output = call(
        early_body, "early", [wide, wide], [features, cotangent, w_self, w_output], flops=2 * flops
    )

    def add_pieces(a_ref, pieces, total):
        for slot, d, p_ref in pieces:
            first = (slot * reps + d) * blocks_dev
            lhs = jnp.concatenate([a_ref[first + u] for u in range(blocks_dev)], axis=1)
            total = total + dot(lhs, p_ref[...])
        return total

    late = [(2, d) for d in range(min(2, reps - 1), reps)]
    soon = [(s, d) for s in range(3) for d in range(reps) if (s, d) not in late]
    window = (own, near, far)

    def soon_body(ao_ref, ap_ref, *refs):
        pieces = [(s, d, ref) for (s, d), ref in zip(soon, refs)]
        zero = jnp.zeros((rows, half), F32)
        refs[-2][...] = add_pieces(ao_ref, pieces, zero)
        refs[-1][...] = add_pieces(ap_ref, pieces, zero)

    part = ((rows, half), F32)
    sum_own, sum_pair = call(
        soon_body, "sum_soon", [part, part], [a_own, a_pair] + [window[s][d] for s, d in soon],
        flops=4 * len(soon) * rows * rows * half,
    )

    def late_body(ao_ref, ap_ref, so_ref, sp_ref, *refs):
        pieces = [(s, d, ref) for (s, d), ref in zip(late, refs)]
        refs[-2][...] = add_pieces(ao_ref, pieces, so_ref[...]).astype(BF)
        refs[-1][...] = add_pieces(ap_ref, pieces, sp_ref[...]).astype(BF)

    agg_mine, agg_send = call(
        late_body, "sum_late", [piece, piece],
        [a_own, a_pair, sum_own, sum_pair] + [window[s][d] for s, d in late],
        flops=4 * len(late) * rows * rows * half,
    )
    agg_other = swap(agg_send, "rep", 1)

    def chain_body(am_ref, ao_ref, self_ref, dso_ref, wa_ref, wm_ref,
                   dm_ref, do_ref, first_ref, second_ref, ds_ref, df_ref):
        h = lax.axis_index("rep") & 1
        wa_mine = wa_ref[half_of(h), :]
        wa_other = wa_ref[half_of(1 - h), :]
        pre_first = dot(am_ref[...], wa_mine) + dot(ao_ref[...], wa_other) + self_ref[...]
        sig = jax.nn.sigmoid(pre_first)
        slope_first = sig * (1.0 + pre_first * (1.0 - sig))
        first = (pre_first * sig).astype(BF)
        first_ref[...] = first
        pre_second = dot(first, wm_ref[...])
        sig = jax.nn.sigmoid(pre_second)
        second_ref[...] = (pre_second * sig).astype(BF)
        ds = (dso_ref[...] * (sig * (1.0 + pre_second * (1.0 - sig)))).astype(BF)
        ds_ref[...] = ds
        df = (dot_nt(ds, wm_ref[...]) * slope_first).astype(BF)
        df_ref[...] = df
        do_ref[...] = dot_nt(df, wa_other).astype(BF)
        dm_ref[...] = dot_nt(df, wa_mine).astype(BF)

    node = ((rows, width), BF)
    del_mine, del_send, first, second, delta_second, delta_first = call(
        chain_body, "chain", [piece, piece, node, node, node, node],
        [agg_mine, agg_other, from_self, from_output, w_aggregate, w_middle], flops=4 * flops,
    )
    del_pair = swap(del_send, "rep", 1)

    def grads_body(f_ref, c_ref, am_ref, ao_ref, first_ref, second_ref, ds_ref, df_ref, keep_ref, send_ref):
        core = lax.axis_index("row") & 1
        h = lax.axis_index("rep") & 1

        def put(number, where, value):
            value = value.astype(BF)

            @pl.when(core == number // 2)
            def _():
                keep_ref[number % 2, where, :] = value

            @pl.when(core != number // 2)
            def _():
                send_ref[number % 2, where, :] = value

        every = pl.ds(0, width)
        df = df_ref[...]
        put(0, every, dot_tn(second_ref[...], c_ref[...]))
        put(1, every, dot_tn(first_ref[...], ds_ref[...]))
        put(2, half_of(h), dot_tn(am_ref[...], df))
        put(2, half_of(1 - h), dot_tn(ao_ref[...], df))
        put(3, every, dot_tn(f_ref[...], df))

    pair_grads = ((2, width, width), BF)
    keep, send = call(
        grads_body, "grads", [pair_grads, pair_grads],
        [features, cotangent, agg_mine, agg_other, first, second, delta_second, delta_first],
        flops=4 * flops,
    )
    got = swap(send, "row", 1)

    def ends_body(f_ref, c_ref, second_ref, df_ref, wo_ref, ws_ref, up_ref, gs_ref):
        up_ref[...] = (f_ref[...].astype(F32) + dot(second_ref[...], wo_ref[...])).astype(BF)
        gs_ref[...] = c_ref[...].astype(F32) + dot_nt(df_ref[...], ws_ref[...])

    updated, grad_base = call(
        ends_body, "ends", [node, wide],
        [features, cotangent, second, delta_first, w_output, w_self], flops=2 * flops,
    )

    def spread_body(slots):
        def body(ao_ref, ap_ref, dm_ref, dp_ref, *outs):
            dm = dm_ref[...]
            dp = dp_ref[...]
            for n, (s, d) in enumerate(slots):
                first = (s * reps + d) * blocks_dev
                here = pl.ds(first, blocks_dev)
                left = ao_ref[here].reshape(rows, rows)
                right = ap_ref[here].reshape(rows, rows)
                outs[n][...] = (dot(left, dm) + dot(right, dp)).astype(BF)
        return body

    def spread(slots, name):
        return call(
            spread_body(slots), name, [piece] * len(slots), [at_own, at_pair, del_mine, del_pair],
            flops=4 * len(slots) * rows * rows * half,
        )

    order = list(range(reps - 1, -1, -1))
    far_out = spread([(2, d) for d in order], "spread_far")
    rest = spread([(1, d) for d in order] + [(0, d) for d in order], "spread_near")
    far_in = [swap_off(v) for v in far_out]
    near_in = [swap(v, "row", 1) for v in rest[:reps]]
    own_sum = rest[reps:]

    def add3_body(a_ref, b_ref, c_ref, o_ref):
        o_ref[...] = (a_ref[...].astype(F32) + b_ref[...].astype(F32) + c_ref[...].astype(F32)).astype(o_ref.dtype)

    home = [None] * reps
    for n, d in enumerate(order):
        total = call(add3_body, "add_panel", [part if d == 0 else piece], [own_sum[n], near_in[n], far_in[n]])[0]
        home[d] = total if d == 0 else swap(total, "rep", d)

    def features_body(g_ref, *refs):
        h = lax.axis_index("rep") & 1
        out = refs[-1]
        for odd in range(2):
            total = g_ref[:, half_of(h ^ odd)]
            for d in range(odd, reps, 2):
                total = total + refs[d][...].astype(F32)
            out[:, half_of(h ^ odd)] = total.astype(BF)

    grad_features = call(features_body, "grad_features", [node], [grad_base] + home)[0]

    flips = [2 * d for d in range(chips)]
    share = ((reps, share_rows, width), BF)

    def share_at(number):
        start = lax.rem(number, chips // 2) * share_rows
        return number // (chips // 2), start

    def pack_body(k_ref, g_ref, *outs):
        r = lax.axis_index("rep")
        chip = lax.axis_index("row") // 2
        for n in range(chips):
            which, start = share_at(chip ^ n)
            for e in range(reps):
                here = pl.ds(pl.multiple_of((r ^ e) * level_rows + start, share_rows), share_rows)
                outs[n][e] = (
                    k_ref[which, here, :].astype(F32) + g_ref[which, here, :].astype(F32)
                ).astype(BF)

    packs = call(pack_body, "pack", [share] * chips, [keep, got])
    planes = [packs[0]] + [swap(packs[n], "row", flips[n]) for n in range(1, chips)]

    def plane_body(*refs):
        ins, outs = refs[:chips], refs[chips:]
        for e in range(reps):
            total = ins[0][e].astype(F32)
            for n in range(1, chips):
                total = total + ins[n][e].astype(F32)
            outs[e][...] = total.astype(BF)

    small = ((share_rows, width), BF)
    levels = call(plane_body, "plane_sum", [small] * reps, planes)
    levels = [levels[0]] + [swap(levels[e], "rep", e) for e in range(1, reps)]

    def level_body(*refs):
        total = refs[0][...].astype(F32)
        for e in range(1, reps):
            total = total + refs[e][...].astype(F32)
        refs[-1][...] = total.astype(BF)

    mine = call(level_body, "level_sum", [small], levels)[0]
    gathered = [mine] + [swap(mine, "row", flips[n]) for n in range(1, chips)]
    others = [swap(v, "row", 1) for v in gathered]

    def out_body(*refs):
        ours, theirs, outs = refs[:chips], refs[chips : 2 * chips], refs[2 * chips :]
        chip = lax.axis_index("row") // 2
        core = lax.axis_index("row") & 1
        for n in range(chips):
            which, start = share_at(chip ^ n)
            here = pl.ds(pl.multiple_of(start, share_rows), share_rows)
            for side, source in ((core, ours), (1 - core, theirs)):
                value = source[n][...].astype(F32) * scale
                for number in range(4):
                    @pl.when(side * 2 + which == number)
                    def _(number=number, value=value):
                        outs[number][here, :] = value

    final = ((level_rows, width), F32)
    totals = call(out_body, "grad_out", [final] * 4, gathered + others)
    return (updated, grad_features, *totals)


def solution(mesh):
    placed = (
        P(("row", "rep"), None),
        P(("row", "rep"), None, None, None),
        P(("row", "rep"), None),
        P(),
        P(),
        P(),
        P(),
        P(("row", "rep"), None),
    )
    return jax.shard_map(
        local,
        mesh=mesh,
        in_specs=placed,
        out_specs=(
            P(("row", "rep"), None),
            P(("row", "rep"), None),
            P("rep", None),
            P("rep", None),
            P("rep", None),
            P("rep", None),
        ),
        check_vma=False,
    )
```

```python
import math

import jax
import jax.numpy as jnp
from jax import lax
from jax.experimental import pallas as pl
from jax.experimental.pallas import tpu as pltpu
from jax.sharding import PartitionSpec as P


BF = jnp.bfloat16
F32 = jnp.float32
VM = pl.BlockSpec(memory_space=pltpu.VMEM)
SM = pl.BlockSpec(memory_space=pltpu.SMEM)


def swap(value, axis, flip):
    count = lax.axis_size(axis)
    return lax.ppermute(value, axis, [(i, i ^ flip) for i in range(count)])


def swap_off(value):
    count = lax.axis_size("row")
    pairs = [(i, (i + 1) % count if i % 2 else (i - 1) % count) for i in range(count)]
    return lax.ppermute(value, "row", pairs)


def nbytes(shape, dtype):
    return math.prod(shape) * jnp.dtype(dtype).itemsize


def call(body, outs, ins, specs=None, flops=0):
    moved = sum(nbytes(o[0], o[1]) for o in outs) + sum(nbytes(i.shape, i.dtype) for i in ins)
    return pl.pallas_call(
        body,
        out_shape=[jax.ShapeDtypeStruct(shape, dtype) for shape, dtype in outs],
        in_specs=specs or [VM] * len(ins),
        out_specs=[VM] * len(outs),
        compiler_params=pltpu.CompilerParams(
            vmem_limit_bytes=min(moved + (8 << 20), 60 << 20)
        ),
        cost_estimate=pl.CostEstimate(flops=flops, bytes_accessed=moved, transcendentals=0),
    )(*ins)


def dot(left, right):
    return jnp.dot(left, right, preferred_element_type=F32)


def dot_nt(left, right):
    return lax.dot_general(left, right, (((1,), (1,)), ((), ())), preferred_element_type=F32)


def dot_tn(left, right):
    return lax.dot_general(left, right, (((0,), (0,)), ((), ())), preferred_element_type=F32)


def layer(features, tiles, columns, w_aggregate, w_self, w_middle, w_output, cotangent):
    blocks_dev, width_k, tile, _ = tiles.shape
    rows, width = features.shape
    half = width // 2
    groups = lax.axis_size("row")
    reps = lax.axis_size("rep")
    chips = groups // 2
    panel_blocks = reps * blocks_dev
    blocks = 3 * panel_blocks
    scale = 1.0 / math.sqrt(rows * groups * reps)
    level_rows = width // reps
    share_rows = 2 * level_rows // chips

    def half_of(offset):
        return pl.ds(pl.multiple_of(offset * half, half), half)

    def split_body(f_ref, mine_ref, other_ref):
        h = lax.axis_index("rep") & 1
        mine_ref[...] = f_ref[:, half_of(h)]
        other_ref[...] = f_ref[:, half_of(1 - h)]

    piece = ((rows, half), BF)
    own_mine, own_other = call(split_body, [piece, piece], [features])

    own = [own_mine] + [None] * (reps - 1)
    for d in range(reps - 1, 0, -1):
        own[d] = swap(own_other if d & 1 else own_mine, "rep", d)
    pair_columns = swap(columns, "rep", 1)
    pair_tiles = swap(tiles, "rep", 1)
    near = [swap(v, "row", 1) for v in own]
    far = [swap_off(v) for v in own]

    def build_body(t_ref, c_ref, a_ref, at_ref):
        g = lax.axis_index("row")
        r = lax.axis_index("rep")
        a_ref[...] = jnp.zeros_like(a_ref)
        at_ref[...] = jnp.zeros_like(at_ref)
        for b in range(blocks_dev):
            for k in range(width_k):
                c = c_ref[b, k]
                within = lax.rem(c, panel_blocks)
                group = lax.div(c, panel_blocks)
                slot = jnp.where(group == g, 0, jnp.where(group == (g ^ 1), 1, 2))
                level = lax.div(within, blocks_dev) ^ r
                index = (slot * reps + level) * blocks_dev + lax.rem(within, blocks_dev)
                t = t_ref[b, k]
                here = pl.ds(b * tile, tile)
                a_ref[index, here, :] += t
                at_ref[index, :, here] += t.T

    adj_shapes = [((blocks, rows, tile), BF), ((blocks, tile, rows), BF)]
    a_own, at_own = call(build_body, adj_shapes, [tiles, columns], [VM, SM])
    a_pair, at_pair = call(build_body, adj_shapes, [pair_tiles, pair_columns], [VM, SM])

    def early_body(f_ref, c_ref, ws_ref, wo_ref, self_ref, dso_ref):
        self_ref[...] = dot(f_ref[...], ws_ref[...])
        dso_ref[...] = dot_nt(c_ref[...], wo_ref[...])

    flops = 2 * rows * width * width
    wide = ((rows, width), F32)
    from_self, from_output = call(
        early_body, [wide, wide], [features, cotangent, w_self, w_output], flops=2 * flops
    )

    def add_pieces(a_ref, pieces, total):
        for slot, d, p_ref in pieces:
            first = (slot * reps + d) * blocks_dev
            lhs = jnp.concatenate([a_ref[first + u] for u in range(blocks_dev)], axis=1)
            total = total + dot(lhs, p_ref[...])
        return total

    late = [(2, d) for d in range(min(2, reps - 1), reps)]
    soon = [(s, d) for s in range(3) for d in range(reps) if (s, d) not in late]
    window = (own, near, far)

    def soon_body(ao_ref, ap_ref, *refs):
        pieces = [(s, d, ref) for (s, d), ref in zip(soon, refs)]
        zero = jnp.zeros((rows, half), F32)
        refs[-2][...] = add_pieces(ao_ref, pieces, zero)
        refs[-1][...] = add_pieces(ap_ref, pieces, zero)

    part = ((rows, half), F32)
    sum_own, sum_pair = call(
        soon_body, [part, part], [a_own, a_pair] + [window[s][d] for s, d in soon],
        flops=4 * len(soon) * rows * rows * half,
    )

    def late_body(ao_ref, ap_ref, so_ref, sp_ref, *refs):
        pieces = [(s, d, ref) for (s, d), ref in zip(late, refs)]
        refs[-2][...] = add_pieces(ao_ref, pieces, so_ref[...]).astype(BF)
        refs[-1][...] = add_pieces(ap_ref, pieces, sp_ref[...]).astype(BF)

    agg_mine, agg_send = call(
        late_body, [piece, piece],
        [a_own, a_pair, sum_own, sum_pair] + [window[s][d] for s, d in late],
        flops=4 * len(late) * rows * rows * half,
    )
    agg_other = swap(agg_send, "rep", 1)

    def chain_body(am_ref, ao_ref, self_ref, dso_ref, wa_ref, wm_ref,
                   dm_ref, do_ref, first_ref, second_ref, ds_ref, df_ref):
        h = lax.axis_index("rep") & 1
        wa_mine = wa_ref[half_of(h), :]
        wa_other = wa_ref[half_of(1 - h), :]
        pre_first = dot(am_ref[...], wa_mine) + dot(ao_ref[...], wa_other) + self_ref[...]
        sig = jax.nn.sigmoid(pre_first)
        slope_first = sig * (1.0 + pre_first * (1.0 - sig))
        first = (pre_first * sig).astype(BF)
        first_ref[...] = first
        pre_second = dot(first, wm_ref[...])
        sig = jax.nn.sigmoid(pre_second)
        second_ref[...] = (pre_second * sig).astype(BF)
        ds = (dso_ref[...] * (sig * (1.0 + pre_second * (1.0 - sig)))).astype(BF)
        ds_ref[...] = ds
        df = (dot_nt(ds, wm_ref[...]) * slope_first).astype(BF)
        df_ref[...] = df
        do_ref[...] = dot_nt(df, wa_other).astype(BF)
        dm_ref[...] = dot_nt(df, wa_mine).astype(BF)

    node = ((rows, width), BF)
    del_mine, del_send, first, second, delta_second, delta_first = call(
        chain_body, [piece, piece, node, node, node, node],
        [agg_mine, agg_other, from_self, from_output, w_aggregate, w_middle], flops=4 * flops,
    )
    del_pair = swap(del_send, "rep", 1)

    def grads_body(f_ref, c_ref, am_ref, ao_ref, first_ref, second_ref, ds_ref, df_ref, keep_ref, send_ref):
        core = lax.axis_index("row") & 1
        h = lax.axis_index("rep") & 1

        def put(number, where, value):
            value = value.astype(BF)

            @pl.when(core == number // 2)
            def _():
                keep_ref[number % 2, where, :] = value

            @pl.when(core != number // 2)
            def _():
                send_ref[number % 2, where, :] = value

        every = pl.ds(0, width)
        df = df_ref[...]
        put(0, every, dot_tn(second_ref[...], c_ref[...]))
        put(1, every, dot_tn(first_ref[...], ds_ref[...]))
        put(2, half_of(h), dot_tn(am_ref[...], df))
        put(2, half_of(1 - h), dot_tn(ao_ref[...], df))
        put(3, every, dot_tn(f_ref[...], df))

    pair_grads = ((2, width, width), BF)
    keep, send = call(
        grads_body, [pair_grads, pair_grads],
        [features, cotangent, agg_mine, agg_other, first, second, delta_second, delta_first],
        flops=4 * flops,
    )
    got = swap(send, "row", 1)

    def ends_body(f_ref, c_ref, second_ref, df_ref, wo_ref, ws_ref, up_ref, gs_ref):
        up_ref[...] = (f_ref[...].astype(F32) + dot(second_ref[...], wo_ref[...])).astype(BF)
        gs_ref[...] = c_ref[...].astype(F32) + dot_nt(df_ref[...], ws_ref[...])

    updated, grad_base = call(
        ends_body, [node, wide],
        [features, cotangent, second, delta_first, w_output, w_self], flops=2 * flops,
    )

    groups_of = (list(range(reps - 1, 1, -1)), [1, 0])
    order = groups_of[0] + groups_of[1]

    def messages(ao_ref, ap_ref, dm, dp, slot, d):
        here = pl.ds((slot * reps + d) * blocks_dev, blocks_dev)
        left = ao_ref[here].reshape(rows, rows)
        right = ap_ref[here].reshape(rows, rows)
        return (dot(left, dm) + dot(right, dp)).astype(BF)

    def spread(slot_lists):
        def body(ao_ref, ap_ref, dm_ref, dp_ref, *outs):
            dm = dm_ref[...]
            dp = dp_ref[...]
            for (slot, levels), out in zip(slot_lists, outs):
                for n, d in enumerate(levels):
                    out[n * rows : (n + 1) * rows] = messages(ao_ref, ap_ref, dm, dp, slot, d)

        return call(
            body, [((len(levels) * rows, half), BF) for _, levels in slot_lists],
            [at_own, at_pair, del_mine, del_pair],
            flops=4 * sum(len(v) for _, v in slot_lists) * rows * rows * half,
        )

    far_out = spread([(2, g) for g in groups_of])
    near_out, own_sum = spread([(1, order), (0, order)])
    far_in = [swap_off(v) for v in far_out]
    near_in = swap(near_out, "row", 1)

    home = [None] * reps
    for i, levels_here in enumerate(groups_of):
        base = len(groups_of[0]) if i else 0

        def add_body(own_ref, near_ref, far_ref, *outs, base=base):
            for n, out in enumerate(outs):
                there = pl.ds((base + n) * rows, rows)
                here = pl.ds(n * rows, rows)
                out[...] = (
                    own_ref[there].astype(F32)
                    + near_ref[there].astype(F32)
                    + far_ref[here].astype(F32)
                ).astype(out.dtype)

        sums = call(
            add_body, [part if d == 0 else piece for d in levels_here],
            [own_sum, near_in, far_in[i]],
        )
        for d, total in zip(levels_here, sums):
            home[d] = total if d == 0 else swap(total, "rep", d)

    def features_body(g_ref, *refs):
        h = lax.axis_index("rep") & 1
        out = refs[-1]
        for odd in range(2):
            total = g_ref[:, half_of(h ^ odd)]
            for d in range(odd, reps, 2):
                total = total + refs[d][...].astype(F32)
            out[:, half_of(h ^ odd)] = total.astype(BF)

    grad_features = call(features_body, [node], [grad_base] + home)[0]

    flips = [2 * d for d in range(chips)]
    cut = width // 2
    share = ((reps, share_rows, cut), BF)
    slab = ((2, level_rows, cut), BF)

    def share_at(number):
        start = lax.rem(number, chips // 2) * share_rows
        return number // (chips // 2), start

    def pack_body(k_ref, g_ref, *outs):
        r = lax.axis_index("rep")
        chip = lax.axis_index("row") // 2
        for e in range(reps):
            first = pl.multiple_of((r ^ e) * level_rows, level_rows)
            for n in range(chips):
                which, start = share_at(chip ^ n)
                here = pl.ds(pl.multiple_of(first + start, share_rows), share_rows)
                outs[n][e] = (
                    k_ref[which, here, :cut].astype(F32) + g_ref[which, here, :cut].astype(F32)
                ).astype(BF)
            here = pl.ds(first, level_rows)
            for i in range(2):
                outs[chips + e][i] = (
                    k_ref[i, here, cut:].astype(F32) + g_ref[i, here, cut:].astype(F32)
                ).astype(BF)

    packs = call(pack_body, [share] * chips + [slab] * reps, [keep, got])
    planes = [packs[0]] + [swap(packs[n], "row", flips[n]) for n in range(1, chips)]
    slabs = packs[chips:]
    slabs = [slabs[0]] + [swap(slabs[e], "rep", e) for e in range(1, reps)]

    def plane_body(*refs):
        ins, outs = refs[:chips], refs[chips:]
        for e in range(reps):
            total = ins[0][e].astype(F32)
            for n in range(1, chips):
                total = total + ins[n][e].astype(F32)
            outs[e][...] = total.astype(BF)

    small = ((share_rows, cut), BF)
    levels = call(plane_body, [small] * reps, planes)
    levels = [levels[0]] + [swap(levels[e], "rep", e) for e in range(1, reps)]

    def level_body(*refs):
        total = refs[0][...].astype(F32)
        for ref in refs[1:-1]:
            total = total + ref[...].astype(F32)
        refs[-1][...] = total.astype(BF)

    mine = call(level_body, [small], levels)[0]
    gathered = [mine] + [swap(mine, "row", flips[n]) for n in range(1, chips)]
    others = [swap(v, "row", 1) for v in gathered]

    slab_sum = call(level_body, [slab], slabs)[0]
    spans = [slab_sum] + [swap(slab_sum, "row", flips[n]) for n in range(1, chips)]

    def span_body(*refs):
        terms = [ref[...].astype(F32) for ref in refs[:-1]]
        while len(terms) > 1:
            terms = [a + b for a, b in zip(terms[::2], terms[1::2])]
        refs[-1][...] = terms[0].astype(BF)

    span = call(span_body, [slab], spans)[0]
    span_other = swap(span, "row", 1)

    def out_body(*refs):
        ours, theirs, outs = refs[:chips], refs[chips : 2 * chips], refs[2 * chips + 2 :]
        chip = lax.axis_index("row") // 2
        core = lax.axis_index("row") & 1

        def put(number, where, columns_here, value):
            for fixed in range(4):
                @pl.when(number == fixed)
                def _(fixed=fixed):
                    outs[fixed][where, columns_here] = value

        for side, source, slab_ref in (
            (core, ours, refs[2 * chips]), (1 - core, theirs, refs[2 * chips + 1])
        ):
            for n in range(chips):
                which, start = share_at(chip ^ n)
                here = pl.ds(pl.multiple_of(start, share_rows), share_rows)
                put(side * 2 + which, here, pl.ds(0, cut), source[n][...].astype(F32) * scale)
            for i in range(2):
                put(
                    side * 2 + i, pl.ds(0, level_rows), pl.ds(cut, width - cut),
                    slab_ref[i].astype(F32) * scale,
                )

    final = ((level_rows, width), F32)
    totals = call(out_body, [final] * 4, gathered + others + [span, span_other])
    return (updated, grad_features, *totals)


def solution(mesh):
    placed = (
        P(("row", "rep"), None),
        P(("row", "rep"), None, None, None),
        P(("row", "rep"), None),
        P(),
        P(),
        P(),
        P(),
        P(("row", "rep"), None),
    )
    return jax.shard_map(
        layer,
        mesh=mesh,
        in_specs=placed,
        out_specs=(
            P(("row", "rep"), None),
            P(("row", "rep"), None),
            P("rep", None),
            P("rep", None),
            P("rep", None),
            P("rep", None),
        ),
        check_vma=False,
    )
```

```python
import math

import jax
import jax.numpy as jnp
from jax import lax
from jax.experimental import pallas as pl
from jax.experimental.pallas import tpu as pltpu
from jax.sharding import PartitionSpec as P


BF = jnp.bfloat16
F32 = jnp.float32
VM = pl.BlockSpec(memory_space=pltpu.VMEM)
SM = pl.BlockSpec(memory_space=pltpu.SMEM)


def swap(value, axis, flip):
    count = lax.axis_size(axis)
    return lax.ppermute(value, axis, [(i, i ^ flip) for i in range(count)])


def swap_off(value):
    count = lax.axis_size("row")
    pairs = [(i, (i + 1) % count if i % 2 else (i - 1) % count) for i in range(count)]
    return lax.ppermute(value, "row", pairs)


def span_flips(chips):
    return [2 << t for t in range(chips.bit_length() - 1)]


def nbytes(shape, dtype):
    return math.prod(shape) * jnp.dtype(dtype).itemsize


def call(body, outs, ins, specs=None, flops=0):
    moved = sum(nbytes(o[0], o[1]) for o in outs) + sum(nbytes(i.shape, i.dtype) for i in ins)
    return pl.pallas_call(
        body,
        out_shape=[jax.ShapeDtypeStruct(shape, dtype) for shape, dtype in outs],
        in_specs=specs or [VM] * len(ins),
        out_specs=[VM] * len(outs),
        compiler_params=pltpu.CompilerParams(
            vmem_limit_bytes=min(moved + (8 << 20), 60 << 20)
        ),
        cost_estimate=pl.CostEstimate(flops=flops, bytes_accessed=moved, transcendentals=0),
    )(*ins)


def dot(left, right):
    return jnp.dot(left, right, preferred_element_type=F32)


def dot_nt(left, right):
    return lax.dot_general(left, right, (((1,), (1,)), ((), ())), preferred_element_type=F32)


def dot_tn(left, right):
    return lax.dot_general(left, right, (((0,), (0,)), ((), ())), preferred_element_type=F32)


def layer(features, tiles, columns, w_aggregate, w_self, w_middle, w_output, cotangent):
    blocks_dev, width_k, tile, _ = tiles.shape
    rows, width = features.shape
    half = width // 2
    groups = lax.axis_size("row")
    reps = lax.axis_size("rep")
    chips = groups // 2
    panel_blocks = reps * blocks_dev
    blocks = 3 * panel_blocks
    scale = 1.0 / math.sqrt(rows * groups * reps)
    level_rows = width // reps
    share_rows = 2 * level_rows // chips

    def half_of(offset):
        return pl.ds(pl.multiple_of(offset * half, half), half)

    def split_body(f_ref, mine_ref, other_ref):
        h = lax.axis_index("rep") & 1
        mine_ref[...] = f_ref[:, half_of(h)]
        other_ref[...] = f_ref[:, half_of(1 - h)]

    piece = ((rows, half), BF)
    own_mine, own_other = call(split_body, [piece, piece], [features])

    own = [own_mine] + [None] * (reps - 1)
    for d in range(reps - 1, 0, -1):
        own[d] = swap(own_other if d & 1 else own_mine, "rep", d)
    pair_columns = swap(columns, "rep", 1)
    pair_tiles = swap(tiles, "rep", 1)
    near = [swap(v, "row", 1) for v in own]
    far = [swap_off(v) for v in own]

    def build_body(turned):
        def body(t_ref, c_ref, *outs):
            g = lax.axis_index("row")
            r = lax.axis_index("rep")
            for out in outs:
                out[...] = jnp.zeros_like(out)
            for b in range(blocks_dev):
                for k in range(width_k):
                    c = c_ref[b, k]
                    within = lax.rem(c, panel_blocks)
                    group = lax.div(c, panel_blocks)
                    slot = jnp.where(group == g, 0, jnp.where(group == (g ^ 1), 1, 2))
                    level = lax.div(within, blocks_dev) ^ r
                    index = (slot * reps + level) * blocks_dev + lax.rem(within, blocks_dev)
                    t = t_ref[b, k]
                    here = pl.ds(b * tile, tile)
                    for out, turn in zip(outs, turned):
                        if turn:
                            out[index, :, here] += t.T
                        else:
                            out[index, here, :] += t

        return body

    plain = ((blocks, rows, tile), BF)
    turned = ((blocks, tile, rows), BF)
    a_own, at_own = call(build_body((False, True)), [plain, turned], [tiles, columns], [VM, SM])
    pair = [pair_tiles, pair_columns]
    a_pair = call(build_body((False,)), [plain], pair, [VM, SM])[0]
    at_pair = call(build_body((True,)), [turned], pair, [VM, SM])[0]

    def early_body(f_ref, c_ref, ws_ref, wo_ref, self_ref, dso_ref):
        self_ref[...] = dot(f_ref[...], ws_ref[...])
        dso_ref[...] = dot_nt(c_ref[...], wo_ref[...])

    flops = 2 * rows * width * width
    wide = ((rows, width), F32)
    from_self, from_output = call(
        early_body, [wide, wide], [features, cotangent, w_self, w_output], flops=2 * flops
    )

    window = own + near + far

    def sum_body(a_ref, *refs):
        total = jnp.zeros((rows, half), F32)
        for n, p_ref in enumerate(refs[:-1]):
            lhs = jnp.concatenate([a_ref[n * blocks_dev + u] for u in range(blocks_dev)], axis=1)
            total = total + dot(lhs, p_ref[...])
        refs[-1][...] = total.astype(BF)

    part = ((rows, half), F32)
    work = 2 * len(window) * rows * rows * half
    agg_send = call(sum_body, [piece], [a_pair] + window, flops=work)[0]
    agg_mine = call(sum_body, [piece], [a_own] + window, flops=work)[0]
    agg_other = swap(agg_send, "rep", 1)

    def chain_body(am_ref, ao_ref, self_ref, dso_ref, wa_ref, wm_ref,
                   dm_ref, do_ref, first_ref, second_ref, ds_ref, df_ref):
        h = lax.axis_index("rep") & 1
        wa_mine = wa_ref[half_of(h), :]
        wa_other = wa_ref[half_of(1 - h), :]
        pre_first = dot(am_ref[...], wa_mine) + dot(ao_ref[...], wa_other) + self_ref[...]
        sig = jax.nn.sigmoid(pre_first)
        slope_first = sig * (1.0 + pre_first * (1.0 - sig))
        first = (pre_first * sig).astype(BF)
        first_ref[...] = first
        pre_second = dot(first, wm_ref[...])
        sig = jax.nn.sigmoid(pre_second)
        second_ref[...] = (pre_second * sig).astype(BF)
        ds = (dso_ref[...] * (sig * (1.0 + pre_second * (1.0 - sig)))).astype(BF)
        ds_ref[...] = ds
        df = (dot_nt(ds, wm_ref[...]) * slope_first).astype(BF)
        df_ref[...] = df
        do_ref[...] = dot_nt(df, wa_other).astype(BF)
        dm_ref[...] = dot_nt(df, wa_mine).astype(BF)

    node = ((rows, width), BF)
    del_mine, del_send, first, second, delta_second, delta_first = call(
        chain_body, [piece, piece, node, node, node, node],
        [agg_mine, agg_other, from_self, from_output, w_aggregate, w_middle], flops=4 * flops,
    )
    del_pair = swap(del_send, "rep", 1)

    def grads_body(sent):
        def body(f_ref, c_ref, am_ref, ao_ref, first_ref, second_ref, ds_ref, df_ref, out_ref):
            core = lax.axis_index("row") & 1
            h = lax.axis_index("rep") & 1

            @pl.when(core == (1 if sent else 0))
            def _():
                out_ref[0] = dot_tn(second_ref[...], c_ref[...]).astype(BF)
                out_ref[1] = dot_tn(first_ref[...], ds_ref[...]).astype(BF)

            @pl.when(core == (0 if sent else 1))
            def _():
                df = df_ref[...]
                out_ref[0, half_of(h), :] = dot_tn(am_ref[...], df).astype(BF)
                out_ref[0, half_of(1 - h), :] = dot_tn(ao_ref[...], df).astype(BF)
                out_ref[1] = dot_tn(f_ref[...], df).astype(BF)

        return body

    pair_grads = ((2, width, width), BF)
    nodes = [features, cotangent, agg_mine, agg_other, first, second, delta_second, delta_first]
    send = call(grads_body(True), [pair_grads], nodes, flops=2 * flops)[0]
    got = swap(send, "row", 1)
    keep = call(grads_body(False), [pair_grads], nodes, flops=2 * flops)[0]

    def ends_body(f_ref, c_ref, second_ref, df_ref, wo_ref, ws_ref, up_ref, gs_ref):
        up_ref[...] = (f_ref[...].astype(F32) + dot(second_ref[...], wo_ref[...])).astype(BF)
        gs_ref[...] = c_ref[...].astype(F32) + dot_nt(df_ref[...], ws_ref[...])

    updated, grad_base = call(
        ends_body, [node, wide],
        [features, cotangent, second, delta_first, w_output, w_self], flops=2 * flops,
    )

    groups_of = (list(range(reps - 1, 1, -1)), [1, 0])
    order = groups_of[0] + groups_of[1]

    def messages(ao_ref, ap_ref, dm, dp, slot, d):
        here = pl.ds((slot * reps + d) * blocks_dev, blocks_dev)
        left = ao_ref[here].reshape(rows, rows)
        right = ap_ref[here].reshape(rows, rows)
        return (dot(left, dm) + dot(right, dp)).astype(BF)

    def spread(slot_lists):
        def body(ao_ref, ap_ref, dm_ref, dp_ref, *outs):
            dm = dm_ref[...]
            dp = dp_ref[...]
            for (slot, levels), out in zip(slot_lists, outs):
                for n, d in enumerate(levels):
                    out[n * rows : (n + 1) * rows] = messages(ao_ref, ap_ref, dm, dp, slot, d)

        return call(
            body, [((len(levels) * rows, half), BF) for _, levels in slot_lists],
            [at_own, at_pair, del_mine, del_pair],
            flops=4 * sum(len(v) for _, v in slot_lists) * rows * rows * half,
        )

    far_out = spread([(2, g) for g in groups_of])
    near_out, own_sum = spread([(1, order), (0, order)])
    far_in = [swap_off(v) for v in far_out]
    near_in = swap(near_out, "row", 1)

    home = [None] * reps
    for i, levels_here in enumerate(groups_of):
        base = len(groups_of[0]) if i else 0

        def add_body(own_ref, near_ref, far_ref, *outs, base=base):
            for n, out in enumerate(outs):
                there = pl.ds((base + n) * rows, rows)
                here = pl.ds(n * rows, rows)
                out[...] = (
                    own_ref[there].astype(F32)
                    + near_ref[there].astype(F32)
                    + far_ref[here].astype(F32)
                ).astype(out.dtype)

        sums = call(
            add_body, [part if d == 0 else piece for d in levels_here],
            [own_sum, near_in, far_in[i]],
        )
        for d, total in zip(levels_here, sums):
            home[d] = total if d == 0 else swap(total, "rep", d)

    def features_body(g_ref, *refs):
        h = lax.axis_index("rep") & 1
        out = refs[-1]
        for odd in range(2):
            total = g_ref[:, half_of(h ^ odd)]
            for d in range(odd, reps, 2):
                total = total + refs[d][...].astype(F32)
            out[:, half_of(h ^ odd)] = total.astype(BF)

    grad_features = call(features_body, [node], [grad_base] + home)[0]

    flips = [2 * d for d in range(chips)]
    cut = width // 2
    share = ((reps, share_rows, cut), BF)

    def stack(count):
        return ((count, 2, level_rows, cut), BF)

    bits = [1 << t for t in range(reps.bit_length() - 1)]
    kept = [e for e in range(reps) if not e & bits[0]]
    sent = [e for e in range(reps) if e & bits[0]]

    def share_at(number):
        start = lax.rem(number, chips // 2) * share_rows
        return number // (chips // 2), start

    def pack_body(k_ref, g_ref, *outs):
        r = lax.axis_index("rep")
        chip = lax.axis_index("row") // 2
        for e in range(reps):
            first = pl.multiple_of((r ^ e) * level_rows, level_rows)
            for n in range(chips):
                which, start = share_at(chip ^ n)
                here = pl.ds(pl.multiple_of(first + start, share_rows), share_rows)
                outs[n][e] = (
                    k_ref[which, here, :cut].astype(F32) + g_ref[which, here, :cut].astype(F32)
                ).astype(BF)
            here = pl.ds(first, level_rows)
            side, place = (kept, 0) if e in kept else (sent, 1)
            for i in range(2):
                outs[chips + place][side.index(e), i] = (
                    k_ref[i, here, cut:].astype(F32) + g_ref[i, here, cut:].astype(F32)
                ).astype(BF)

    packs = call(pack_body, [share] * chips + [stack(len(kept)), stack(len(sent))], [keep, got])
    planes = [packs[0]] + [swap(packs[n], "row", flips[n]) for n in range(1, chips)]

    slab_keep = packs[chips]
    slab_in = swap(packs[chips + 1], "rep", bits[0])
    for bit in bits[1:]:
        stay = [n for n, e in enumerate(kept) if not e & bit]
        leave = [n for n, e in enumerate(kept) if e & bit]

        def halve_body(own_ref, in_ref, stay_ref, leave_ref, stay=stay, leave=leave):
            for out, numbers in ((stay_ref, stay), (leave_ref, leave)):
                for n, source in enumerate(numbers):
                    out[n] = (own_ref[source].astype(F32) + in_ref[source].astype(F32)).astype(BF)

        slab_keep, slab_send = call(
            halve_body, [stack(len(stay)), stack(len(leave))], [slab_keep, slab_in]
        )
        kept = [kept[n] for n in stay]
        slab_in = swap(slab_send, "rep", bit)

    def plane_body(*refs):
        ins, outs = refs[:chips], refs[chips:]
        for e in range(reps):
            total = ins[0][e].astype(F32)
            for n in range(1, chips):
                total = total + ins[n][e].astype(F32)
            outs[e][...] = total.astype(BF)

    small = ((share_rows, cut), BF)
    levels = call(plane_body, [small] * reps, planes)
    levels = [levels[0]] + [swap(levels[e], "rep", e) for e in range(1, reps)]

    def level_body(*refs):
        total = refs[0][...].astype(F32)
        for ref in refs[1:-1]:
            total = total + ref[...].astype(F32)
        refs[-1][...] = total.astype(BF)

    mine = call(level_body, [small], levels)[0]
    gathered = [mine] + [swap(mine, "row", flips[n]) for n in range(1, chips)]
    others = [swap(v, "row", 1) for v in gathered]

    def span_body(a_ref, b_ref, out_ref):
        out_ref[...] = (a_ref[...].astype(F32) + b_ref[...].astype(F32)).astype(BF)

    span = call(span_body, [stack(1)], [slab_keep, slab_in])[0]
    for flip in reversed(span_flips(chips)):
        moved = swap(span, "row", flip)
        span = call(span_body, [stack(1)], [span, moved])[0]
    span_other = swap(span, "row", 1)

    def out_body(*refs):
        ours, theirs, outs = refs[:chips], refs[chips : 2 * chips], refs[2 * chips + 2 :]
        chip = lax.axis_index("row") // 2
        core = lax.axis_index("row") & 1

        def put(number, where, columns_here, value):
            for fixed in range(4):
                @pl.when(number == fixed)
                def _(fixed=fixed):
                    outs[fixed][where, columns_here] = value

        for side, source, slab_ref in (
            (core, ours, refs[2 * chips]), (1 - core, theirs, refs[2 * chips + 1])
        ):
            for n in range(chips):
                which, start = share_at(chip ^ n)
                here = pl.ds(pl.multiple_of(start, share_rows), share_rows)
                put(side * 2 + which, here, pl.ds(0, cut), source[n][...].astype(F32) * scale)
            for i in range(2):
                put(
                    side * 2 + i, pl.ds(0, level_rows), pl.ds(cut, width - cut),
                    slab_ref[0, i].astype(F32) * scale,
                )

    final = ((level_rows, width), F32)
    totals = call(out_body, [final] * 4, gathered + others + [span, span_other])
    return (updated, grad_features, *totals)


def solution(mesh):
    placed = (
        P(("row", "rep"), None),
        P(("row", "rep"), None, None, None),
        P(("row", "rep"), None),
        P(),
        P(),
        P(),
        P(),
        P(("row", "rep"), None),
    )
    return jax.shard_map(
        layer,
        mesh=mesh,
        in_specs=placed,
        out_specs=(
            P(("row", "rep"), None),
            P(("row", "rep"), None),
            P("rep", None),
            P("rep", None),
            P("rep", None),
            P("rep", None),
        ),
        check_vma=False,
    )
```
